32 devices in a mesh: wide: 8 (over z, x), narrow: 4 (over y, core).
Axes of the slice: x: 2, y: 2, z: 4, core: 2. Of those that a mesh axis runs over, the one named last changes fastest.
Arguments:
- factors: bfloat16 [192, 256, 768], P(('wide', 'narrow')), may hold values from -0.21875 to 0.21875
- integrals: bfloat16 [192, 256, 768], P(('wide', 'narrow')), may hold values from -6 to 6
- pao_energy: float32 [192, 256], replicated, may hold values from 0.3 to 4
- lmo_energy: float32 [192], replicated, may hold values from -1.5 to -0.3
- partners: int32 [192, 4], replicated, may hold values from 0 to 191, as said below
Outputs:
- auxiliary_density: float32 [768, 768], P('wide', 'narrow')
The draws below stay inside these ranges and needn't reach their ends.
Inputs may be any that keep to these rules, and one draw needn't show every extreme that they name: LMO i is held by device i // 6, devices counted with wide outermost. Each LMO's 4 partners are LMOs other than itself, held by devices with the same narrow index as its own holder, in 4 different wide groups (its own device may be one). The listed pairs of one device's 6 LMOs point to exactly 8 devices, with exactly 3 pairs and exactly 2 distinct partners on each of them.
All inputs are finite; a program needn't handle non-finite values.
Results may differ from the reference program's by a relative error of at most 0.0035.
Values may be sent and summed in bfloat16 or wider, within the bound.
No kernel may reach another device: no remote copies, remote signals or barrier semaphores. Data moves between devices by JAX's collectives and lax.ppermute only.
A program may use at most 128 MiB of HBM per device.

```python
import math
import jax
import jax.numpy as jnp
from jax import lax

LMO_DEV = 6
PARTNERS = 4
PAO = 256
AUX = 768
LMOS = 192
N_WIDE = 8
N_NARROW = 4
DEVICES = 32


def draw_partners(key, part):
    device_count = N_WIDE * N_NARROW
    half = LMO_DEV // 2
    groups = 2 * PARTNERS
    subkeys = jax.random.split(jax.random.fold_in(key, 11), 6)
    offsets = jax.vmap(lambda subkey: jax.random.permutation(subkey, N_WIDE))(jax.random.split(subkeys[0], device_count))[:, :groups].astype(jnp.int32)
    slot_order = jax.vmap(lambda subkey: jax.random.permutation(subkey, LMO_DEV))(jax.random.split(subkeys[1], device_count)).astype(jnp.int32)
    partner_order = jax.vmap(lambda subkey: jax.random.permutation(subkey, PARTNERS))(jax.random.split(subkeys[2], device_count * LMO_DEV)).astype(jnp.int32)
    partner_order = partner_order.reshape(device_count, LMO_DEV, PARTNERS)
    odd_member = jax.random.randint(subkeys[3], (device_count, groups), 0, 3, dtype=jnp.int32)
    pick = jax.random.randint(subkeys[4], (device_count, groups), 0, LMO_DEV, dtype=jnp.int32)
    stride = jax.random.randint(subkeys[5], (device_count, groups), 1, LMO_DEV, dtype=jnp.int32)
    device_ids = jnp.arange(device_count, dtype=jnp.int32)
    target = (device_ids[:, None] // N_NARROW + offsets) % N_WIDE
    owner = target * N_NARROW + (device_ids % N_NARROW)[:, None]
    side = jnp.arange(groups, dtype=jnp.int32) // PARTNERS
    member = jnp.arange(3, dtype=jnp.int32)
    triple = slot_order[:, side[:, None] * half + member[None, :]]
    others = slot_order[:, (1 - side)[:, None] * half + member[None, :]]
    first_local = jnp.take_along_axis(others, (pick % 3)[:, :, None], axis=2)[:, :, 0]
    second_local = jnp.take_along_axis(others, ((pick % 3 + 1 + stride % 2) % 3)[:, :, None], axis=2)[:, :, 0]
    same_device = offsets == 0
    first_local = jnp.where(same_device, first_local, pick)
    second_local = jnp.where(same_device, second_local, (pick + stride) % LMO_DEV)
    chosen = jnp.where(member[None, None, :] == odd_member[:, :, None], second_local[:, :, None], first_local[:, :, None])
    values = owner[:, :, None] * LMO_DEV + chosen
    flat_slots = triple.reshape(device_count, groups * 3)
    column_pos = jnp.broadcast_to((jnp.arange(groups, dtype=jnp.int32) % PARTNERS)[None, :, None], (device_count, groups, 3)).reshape(device_count, groups * 3)
    rows = jnp.take_along_axis(partner_order, flat_slots[:, :, None], axis=1)
    columns = jnp.take_along_axis(rows, column_pos[:, :, None], axis=2)[:, :, 0]
    table = jnp.zeros((device_count, LMO_DEV, PARTNERS), jnp.int32)
    table = table.at[device_ids[:, None], flat_slots, columns].set(values.reshape(device_count, groups * 3))
    return table.reshape(device_count * LMO_DEV, PARTNERS)


def block_scale(rng, shape, pieces, smallest, high):
    def one(position, blocks):
        heights = jax.random.uniform(jax.random.fold_in(jax.random.fold_in(rng, 6), position), (blocks,), jnp.float32, smallest / len(pieces), high / len(pieces))
        return jnp.repeat(jnp.exp(heights), shape[position] // blocks).reshape((-1,) + (1,) * (len(shape) - position - 1))

    factor_of = one(*pieces[0])
    for cut in pieces[1:]:
        factor_of = factor_of * one(*cut)
    return factor_of


def gaussian(key, extent, deviation, bound, cuts=(), kind=jnp.bfloat16):
    level = block_scale(key, extent, cuts, -0.22, 0.18) if cuts else 1.0
    values = jax.random.normal(key, extent, jnp.float32) * deviation * level
    return jnp.minimum(jnp.maximum(values, -bound), bound).astype(kind)


def setup_inputs(seed: int = 0) -> dict:
    arg_keys = jax.random.split(jax.random.key(seed), 6)
    factors = gaussian(arg_keys[0], (LMOS, PAO, AUX), (1.3 * (AUX * PAO * PAO * DEVICES) ** -0.16666667), 0.21875, ((0, 32),))
    integrals = gaussian(arg_keys[1], (LMOS, PAO, AUX), 1.0, 6.0, ((0, 32),))
    pao_energy = jnp.clip(jnp.exp(jax.random.uniform(arg_keys[2], (LMOS, PAO), jnp.float32, math.log(0.3), math.log(4.0))), 0.3, 4.0)
    lmo_energy = jnp.clip(jax.random.uniform(arg_keys[3], (LMOS,), jnp.float32, -1.5, -0.3), -1.5, -0.3)
    partners = draw_partners(jax.random.fold_in(arg_keys[5], 71), 0)
    return {"factors": factors, "integrals": integrals, "pao_energy": pao_energy, "lmo_energy": lmo_energy, "partners": partners}


def reference(factors, integrals, pao_energy, lmo_energy, partners):
    block_count = LMOS // LMO_DEV

    def one_block(total, block):
        first_lmo = (block * LMO_DEV).astype(jnp.int32)
        own = lax.dynamic_slice_in_dim(factors, first_lmo, LMO_DEV, 0).astype(jnp.float32)
        resident = lax.dynamic_slice_in_dim(integrals, first_lmo, LMO_DEV, 0)
        listed = lax.dynamic_slice_in_dim(partners, first_lmo, LMO_DEV, 0).astype(jnp.int32)
        other = jnp.take(factors, listed, axis=0).astype(jnp.float32)
        own_pao = lax.dynamic_slice_in_dim(pao_energy, first_lmo, LMO_DEV, 0)
        other_pao = jnp.take(pao_energy, listed, axis=0)
        own_lmo = lax.dynamic_slice_in_dim(lmo_energy, first_lmo, LMO_DEV, 0)
        other_lmo = jnp.take(lmo_energy, listed, axis=0)
        denominator = (own_pao[:, None, :, None] + other_pao[:, :, None, :]
                       - own_lmo[:, None, None, None] - other_lmo[:, :, None, None])
        pair_integral = jnp.einsum('sar,skbr->skab', own, other)
        amplitude = (pair_integral / denominator).astype(jnp.bfloat16)
        fitted_density = jnp.einsum('skab,skbr->sar', amplitude.astype(jnp.float32), other).astype(jnp.bfloat16)
        partial_total = jnp.dot(resident.reshape(-1, AUX).T, fitted_density.reshape(-1, AUX),
                                preferred_element_type=jnp.float32)
        return total + partial_total, None

    total, _ = lax.scan(one_block, jnp.zeros((AUX, AUX), jnp.float32),
                        jnp.arange(block_count, dtype=jnp.int32))
    return 0.5 * (total + total.T)
```

```python
import functools

import jax
import jax.numpy as jnp
from jax import lax
from jax.experimental import pallas as pl
from jax.experimental.pallas import tpu as pltpu
from jax.sharding import PartitionSpec as P

PARTNERS = 4
F32 = jnp.float32
BF16 = jnp.bfloat16


def xor_permute(x, axis, bit):
    return lax.ppermute(x, axis, [(i, i ^ bit) for i in range(lax.axis_size(axis))])


def take_kernel(base, rows, index_ref, source_ref, *refs):
    outputs, (buffer, loaded, stored) = refs[:-3], refs[-3:]
    first, count = rows
    loads, stores = [], []
    for k in range(2 * len(outputs)):
        lmo = source_ref.at[index_ref[base + k], pl.ds(first, count), :]
        loads.append(pltpu.make_async_copy(lmo, buffer.at[k], loaded.at[k]))
        target = outputs[k // 2].at[k % 2]
        stores.append(pltpu.make_async_copy(buffer.at[k], target, stored.at[k]))
    for load in loads:
        load.start()
    for load, store in zip(loads, stores):
        load.wait()
        store.start()
    for store in stores:
        store.wait()


def take_pairs(source, index, base, outputs, first, count):
    auxiliary = source.shape[2]
    any_spec = pl.BlockSpec(memory_space=pl.ANY)
    return pl.pallas_call(
        functools.partial(take_kernel, base, (first, count)),
        out_shape=[jax.ShapeDtypeStruct((2, count, auxiliary), source.dtype)] * outputs,
        grid_spec=pltpu.PrefetchScalarGridSpec(
            num_scalar_prefetch=1,
            grid=(1,),
            in_specs=[any_spec],
            out_specs=[any_spec] * outputs,
            scratch_shapes=[
                pltpu.VMEM((2 * outputs, count, auxiliary), source.dtype),
                pltpu.SemaphoreType.DMA((2 * outputs,)),
                pltpu.SemaphoreType.DMA((2 * outputs,)),
            ],
        ),
        cost_estimate=pl.CostEstimate(
            flops=0, transcendentals=0, bytes_accessed=8 * outputs * count * auxiliary
        ),
        name="take_pairs",
    )(index, source)


def pair_kernel(part_count, base, meta_ref, own_ref, own_energy_ref, *refs):
    parts = refs[:part_count]
    energies = refs[part_count : 2 * part_count]
    before_ref, after_ref = refs[2 * part_count :]
    step = pl.program_id(0)
    total = before_ref[0]
    own = own_ref[0]
    own_energy = own_energy_ref[0]
    update = None
    for part_ref, energy_ref in zip(parts, energies):
        part = part_ref[0]
        integral = lax.dot_general(
            own, part, (((1,), (1,)), ((), ())), preferred_element_type=F32
        )
        amplitude = (integral / (own_energy + energy_ref[0])).astype(BF16)
        term = jnp.dot(amplitude, part, preferred_element_type=F32)
        update = term if update is None else update + term
    valid = meta_ref[base + 5 * step] > 0
    after_ref[0] = jnp.where(valid, total + update, total)


def pair_terms(meta, group, factors, own_energy, parts, energies, density):
    lmo_dev, orbitals, auxiliary = factors.shape
    steps = lmo_dev // 2
    base = 5 * steps * group

    def pick(column):
        return lambda k, meta_ref: (meta_ref[base + 5 * k + column], 0, 0)

    in_specs = [
        pl.BlockSpec((1, orbitals, auxiliary), pick(1)),
        pl.BlockSpec((1, orbitals, 1), pick(1)),
    ]
    for part in parts:
        in_specs.append(pl.BlockSpec((1,) + part.shape[1:], pick(2 if part.shape[0] == 2 else 3)))
    for energy in energies:
        in_specs.append(pl.BlockSpec((1,) + energy.shape[1:], pick(4)))
    in_specs.append(pl.BlockSpec((1, orbitals, auxiliary), pick(1)))
    return pl.pallas_call(
        functools.partial(pair_kernel, len(parts), base),
        out_shape=jax.ShapeDtypeStruct(density.shape, F32),
        grid_spec=pltpu.PrefetchScalarGridSpec(
            num_scalar_prefetch=1,
            grid=(steps,),
            in_specs=in_specs,
            out_specs=pl.BlockSpec((1, orbitals, auxiliary), pick(1)),
        ),
        input_output_aliases={len(in_specs): 0},
        cost_estimate=pl.CostEstimate(
            flops=4 * steps * orbitals * orbitals * auxiliary,
            transcendentals=steps * orbitals * orbitals,
            bytes_accessed=12 * steps * orbitals * auxiliary,
        ),
        name="pair_terms",
    )(meta, factors, own_energy, *parts, *energies, density)


def total_kernel(slab, parity_ref, integrals_ref, density_ref, keep_ref, send_ref, total_ref):
    step = pl.program_id(0)
    term = jnp.dot(integrals_ref[...], density_ref[0].astype(BF16), preferred_element_type=F32)

    @pl.when(step == 0)
    def _():
        total_ref[...] = term

    @pl.when(step > 0)
    def _():
        total_ref[...] += term

    @pl.when(step == pl.num_programs(0) - 1)
    def _():
        total = total_ref[...]
        total_ref[...] = 0.5 * (total + total.T)
        parity = parity_ref[0]
        for q in range(keep_ref.shape[0]):
            keep_ref[q] = total_ref[pl.ds((2 * q + parity) * slab, slab), :]
            send_ref[q] = total_ref[pl.ds((2 * q + 1 - parity) * slab, slab), :].astype(BF16)


def symmetric_total(parity, integrals, density, narrow_count):
    lmo_dev, orbitals, auxiliary = density.shape
    slab = auxiliary // narrow_count
    out = (narrow_count // 2, slab, auxiliary)
    full = pl.BlockSpec(out, lambda i, parity_ref: (0, 0, 0))
    return pl.pallas_call(
        functools.partial(total_kernel, slab),
        out_shape=[jax.ShapeDtypeStruct(out, F32), jax.ShapeDtypeStruct(out, BF16)],
        grid_spec=pltpu.PrefetchScalarGridSpec(
            num_scalar_prefetch=1,
            grid=(lmo_dev,),
            in_specs=[
                pl.BlockSpec((auxiliary, orbitals), lambda i, parity_ref: (0, i)),
                pl.BlockSpec((1, orbitals, auxiliary), lambda i, parity_ref: (i, 0, 0)),
            ],
            out_specs=[full, full],
            scratch_shapes=[pltpu.VMEM((auxiliary, auxiliary), F32)],
        ),
        cost_estimate=pl.CostEstimate(
            flops=2 * lmo_dev * orbitals * auxiliary * auxiliary,
            transcendentals=0,
            bytes_accessed=6 * density.size,
        ),
        name="symmetric_total",
    )(parity, integrals, density)


def halve(x, axis, bit):
    pairs = x.reshape((x.shape[0] // 2, 2) + x.shape[1:])
    mine = (lax.axis_index(axis) & bit) // bit
    keep = lax.dynamic_index_in_dim(pairs, mine, 1, keepdims=False)
    send = lax.dynamic_index_in_dim(pairs, 1 - mine, 1, keepdims=False).astype(BF16)
    return keep + xor_permute(send, axis, bit).astype(F32)


def local(factors, integrals, pao_energy, lmo_energy, partners):
    wide_count = lax.axis_size("wide")
    narrow_count = lax.axis_size("narrow")
    wide_index = lax.axis_index("wide")
    narrow_index = lax.axis_index("narrow")
    lmo_dev, orbitals, auxiliary = factors.shape
    pair_count = lmo_dev * PARTNERS
    group_pairs = lmo_dev // 2
    half = wide_count // 2
    chunk = orbitals * 5 // 16 // 16 * 16
    direct = 2 * chunk

    mirrored = [
        xor_permute(factors[:, c * chunk : (c + 1) * chunk], "wide", half) for c in range(2)
    ]

    column = lax.dynamic_index_in_dim(
        partners.reshape(wide_count, narrow_count, pair_count), narrow_index, 1, keepdims=False
    )
    groups = column // lmo_dev // narrow_count
    slots = column % lmo_dev
    ids = jnp.arange(wide_count, dtype=jnp.int32)
    hit = groups[:, :, None] == ids
    low = jnp.min(jnp.where(hit, slots[:, :, None], lmo_dev - 1), axis=1)
    high = jnp.max(jnp.where(hit, slots[:, :, None], 0), axis=1)
    asked = jnp.stack([low, high], axis=-1)
    order = wide_index ^ ids
    by_order = (order[:, None] == ids)[:, :, None]

    def asked_of(group):
        listed = lax.dynamic_index_in_dim(asked, group, 1, keepdims=False)
        return jnp.sum(jnp.where(by_order, listed[None], 0), axis=1, dtype=jnp.int32)

    asked = jnp.stack([asked_of(wide_index), asked_of(wide_index ^ half)]).reshape(-1)

    near = [
        xor_permute(x, "wide", d + 1)
        for d, x in enumerate(take_pairs(factors, asked, 2, half - 1, 0, orbitals))
    ]
    far_asked, first = lax.optimization_barrier((asked, mirrored[0]))
    mirrored[0] = first
    far = [
        xor_permute(x, "wide", half + d)
        for d, x in enumerate(take_pairs(factors, far_asked, 2 * half, half, direct, orbitals - direct))
    ]
    forwarded = [
        [
            xor_permute(x, "wide", d + 1)
            for d, x in enumerate(take_pairs(m, asked, 2 * wide_count + 2, half - 1, 0, chunk))
        ]
        for m in mirrored
    ]

    own_groups = lax.dynamic_index_in_dim(groups, wide_index, 0, keepdims=False)
    own_slots = lax.dynamic_index_in_dim(slots, wide_index, 0, keepdims=False)
    listed = lax.dynamic_index_in_dim(column, wide_index, 0, keepdims=False)
    own_low = lax.dynamic_index_in_dim(low, wide_index, 0, keepdims=False)
    pair_ids = jnp.arange(pair_count, dtype=jnp.int32)
    place = jnp.sum(
        (own_groups[:, None] == own_groups[None, :]) & (pair_ids[None, :] < pair_ids[:, None]),
        axis=1, dtype=jnp.int32,
    )
    steps = jnp.arange(group_pairs, dtype=jnp.int32)
    picked = (own_groups == order[:, None, None]) & (place == steps[None, :, None])

    def of_pair(values):
        return jnp.sum(jnp.where(picked, values, 0), axis=2, dtype=jnp.int32)

    valid = of_pair(jnp.ones_like(pair_ids))
    lmo = jnp.where(valid > 0, of_pair(pair_ids // PARTNERS), steps)
    slot = of_pair(own_slots)
    lowest = jnp.sum(jnp.where(own_groups[:, None] == ids, own_low, 0), axis=1, dtype=jnp.int32)
    rank = of_pair((own_slots > lowest).astype(jnp.int32))
    meta = jnp.stack([valid, lmo, rank, slot, of_pair(listed)], axis=-1).reshape(-1)

    shifted = pao_energy - lmo_energy[:, None]
    first_lmo = (wide_index * narrow_count + narrow_index) * lmo_dev
    own_energy = lax.dynamic_slice_in_dim(shifted, first_lmo, lmo_dev, 0)[:, :, None]
    whole = shifted[:, None, :]
    cut = [whole[:, :, :chunk], whole[:, :, chunk:direct], whole[:, :, direct:]]

    density = jnp.zeros((lmo_dev, orbitals, auxiliary), F32)
    terms = functools.partial(pair_terms)
    density = terms(meta, 0, factors, own_energy, [factors], [whole], density)
    for d in range(1, half):
        density = terms(meta, d, factors, own_energy, [near[d - 1]], [whole], density)
    for d in range(half):
        if d == 0:
            parts = [mirrored[0], mirrored[1], far[0]]
        else:
            parts = [forwarded[0][d - 1], forwarded[1][d - 1], far[d]]
        density = terms(meta, half + d, factors, own_energy, parts, cut, density)

    flipped = integrals.reshape(lmo_dev * orbitals, auxiliary).T
    parity = (narrow_index & 1).astype(jnp.int32).reshape(1)
    keep, send = symmetric_total(parity, flipped, density, narrow_count)

    x = keep + xor_permute(send, "narrow", 1).astype(F32)
    bit = 2
    while bit < narrow_count:
        x = halve(x, "narrow", bit)
        bit *= 2
    tile = (auxiliary // wide_count, auxiliary // narrow_count)
    x = x[0].T.reshape(wide_count, tile[0] * tile[1] // 128, 128)
    bit = 1
    while bit < wide_count:
        x = halve(x, "wide", bit)
        bit *= 2
    return x[0].reshape(tile)


def solution(mesh):
    in_specs = (P(("wide", "narrow"), None, None), P(("wide", "narrow"), None, None), P(), P(), P())
    out_specs = P("wide", "narrow")
    return jax.shard_map(local, mesh=mesh, in_specs=in_specs, out_specs=out_specs, check_vma=False)
```

```python
import functools

import jax
import jax.numpy as jnp
from jax import lax
from jax.experimental import pallas as pl
from jax.experimental.pallas import tpu as pltpu
from jax.sharding import PartitionSpec as P


PARTNERS = 4
F32 = jnp.float32
BF16 = jnp.bfloat16
VMEM_LIMIT = 24 << 20


def xor_permute(x, axis, bit):
    return lax.ppermute(x, axis, [(i, i ^ bit) for i in range(lax.axis_size(axis))])


def take_kernel(base, rows, index_ref, source_ref, *refs):
    outputs, (buffer, loaded, stored) = refs[:-3], refs[-3:]
    first, count = rows
    loads, stores = [], []
    for k in range(2 * len(outputs)):
        lmo = source_ref.at[index_ref[base + k], pl.ds(first, count), :]
        loads.append(pltpu.make_async_copy(lmo, buffer.at[k], loaded.at[k]))
        target = outputs[k // 2].at[k % 2]
        stores.append(pltpu.make_async_copy(buffer.at[k], target, stored.at[k]))
    for load in loads:
        load.start()
    for load, store in zip(loads, stores):
        load.wait()
        store.start()
    for store in stores:
        store.wait()


def take_pairs(source, index, base, outputs, first, count):
    auxiliary = source.shape[2]
    any_spec = pl.BlockSpec(memory_space=pl.ANY)
    return pl.pallas_call(
        functools.partial(take_kernel, base, (first, count)),
        out_shape=[jax.ShapeDtypeStruct((2, count, auxiliary), source.dtype)] * outputs,
        grid_spec=pltpu.PrefetchScalarGridSpec(
            num_scalar_prefetch=1,
            grid=(1,),
            in_specs=[pl.BlockSpec(memory_space=pltpu.HBM)],
            out_specs=[any_spec] * outputs,
            scratch_shapes=[
                pltpu.VMEM((2 * outputs, count, auxiliary), source.dtype),
                pltpu.SemaphoreType.DMA((2 * outputs,)),
                pltpu.SemaphoreType.DMA((2 * outputs,)),
            ],
        ),
        cost_estimate=pl.CostEstimate(
            flops=0, transcendentals=0, bytes_accessed=8 * outputs * count * auxiliary
        ),
        compiler_params=pltpu.CompilerParams(vmem_limit_bytes=VMEM_LIMIT),
        name="take_pairs",
    )(index, source)


def start_all(copies):
    for copy in copies:
        copy.start()


def load_sets(sets, meta_ref, part_refs, buffers, sem):
    copies, part_refs = [], iter(part_refs)
    for (base, _, _, counts), buffer in zip(sets, buffers):
        loads, row = [], 0
        for count in counts:
            part_ref = next(part_refs)
            for r in range(2):
                slot = r if part_ref.shape[0] == 2 else meta_ref[base + r]
                target = buffer.at[r, pl.ds(row, count), :]
                number = sum(len(c) for c in copies) + len(loads)
                loads.append(pltpu.make_async_copy(part_ref.at[slot], target, sem.at[number]))
            row += count
        copies.append(loads)
    return copies


def add_sets(sets, copies, buffers, steps, meta_ref, energy_ref, factors_ref, density_ref):
    for (base, group, first, counts), loads, buffer in zip(sets, copies, buffers):
        for copy in loads:
            copy.wait()
        for k in range(steps):

            @pl.when(meta_ref[base + 2 + 3 * k] > 0)
            def _():
                lmo, rank = meta_ref[base + 3 + 3 * k], meta_ref[base + 4 + 3 * k]
                energy = energy_ref[group]
                own_energy = jnp.broadcast_to(energy[k : k + 1], (8, energy.shape[1])).T[:, :1]
                other = energy[steps + k : steps + k + 1, first : first + sum(counts)]
                part = buffer[rank]
                integral = lax.dot_general(
                    factors_ref[lmo], part, (((1,), (1,)), ((), ())), preferred_element_type=F32
                )
                amplitude = (integral / (own_energy + other)).astype(BF16)
                density_ref[lmo] += jnp.dot(amplitude, part, preferred_element_type=F32)


def pair_kernel(sets, steps, initial, meta_ref, energy_ref, factors_ref, *refs):
    count = sum(len(counts) for *_, counts in sets)
    part_refs, refs = refs[:count], refs[count if initial else count + 1 :]
    density_ref, buffers, sem = refs[0], refs[1:-1], refs[-1]
    copies = load_sets(sets, meta_ref, part_refs, buffers, sem)
    for loads in copies:
        start_all(loads)
    if initial:
        density_ref[...] = jnp.zeros_like(density_ref)
    add_sets(sets, copies, buffers, steps, meta_ref, energy_ref, factors_ref, density_ref)


def set_shapes(sets, steps):
    static = tuple(
        ((2 + 3 * steps) * group, group, first, tuple(part.shape[1] for part in parts))
        for group, parts, first in sets
    )
    return static, [part for _, parts, _ in sets for part in parts]


def set_scratch(static, auxiliary):
    count = sum(2 * len(counts) for *_, counts in static)
    return [
        pltpu.VMEM((2, sum(counts), auxiliary), BF16) for *_, counts in static
    ], pltpu.SemaphoreType.DMA((count,))


def pair_terms(meta, energy, factors, sets, density):
    lmo_dev, orbitals, auxiliary = factors.shape
    steps = lmo_dev // 2
    static, parts = set_shapes(sets, steps)
    initial = density is None
    buffers, sem = set_scratch(static, auxiliary)
    any_spec = pl.BlockSpec(memory_space=pl.ANY)
    vmem_spec = pl.BlockSpec(memory_space=pltpu.VMEM)
    return pl.pallas_call(
        functools.partial(pair_kernel, static, steps, initial),
        out_shape=pltpu.VMEM((lmo_dev, orbitals, auxiliary), F32),
        in_specs=[pl.BlockSpec(memory_space=pltpu.SMEM), vmem_spec, vmem_spec]
        + [any_spec] * len(parts)
        + ([] if initial else [vmem_spec]),
        out_specs=vmem_spec,
        scratch_shapes=buffers + [sem],
        input_output_aliases={} if initial else {3 + len(parts): 0},
        cost_estimate=pl.CostEstimate(
            flops=4 * len(sets) * steps * orbitals * orbitals * auxiliary,
            transcendentals=len(sets) * steps * orbitals * orbitals,
            bytes_accessed=4 * len(sets) * orbitals * auxiliary,
        ),
        compiler_params=pltpu.CompilerParams(vmem_limit_bytes=VMEM_LIMIT),
        name="pair_terms",
    )(meta, energy, factors, *parts, *([] if initial else [density]))


def finish_kernel(sets, steps, slab, meta_ref, parity_ref, energy_ref, factors_ref, *refs):
    count = sum(len(counts) for *_, counts in sets)
    part_refs, refs = refs[:count], refs[count:]
    _, integrals_ref, keep_ref, send_ref, density_ref = refs[:5]
    buffers, (integrals, total, sem, integrals_sem) = refs[5:-4], refs[-4:]
    lmo_dev = density_ref.shape[0]
    copies = load_sets(sets, meta_ref, part_refs, buffers, sem)
    loads = [
        pltpu.make_async_copy(integrals_ref.at[i], integrals.at[i], integrals_sem.at[i])
        for i in range(lmo_dev)
    ]
    for group in copies:
        start_all(group)
    start_all(loads)
    add_sets(sets, copies, buffers, steps, meta_ref, energy_ref, factors_ref, density_ref)
    for i in range(lmo_dev):
        loads[i].wait()
        term = lax.dot_general(
            integrals[i], density_ref[i].astype(BF16), (((0,), (0,)), ((), ())),
            preferred_element_type=F32,
        )
        if i == 0:
            total[...] = term
        else:
            total[...] += term
    value = total[...]
    total[...] = 0.5 * (value + value.T)
    parity = parity_ref[0]
    for q in range(keep_ref.shape[0]):
        keep_ref[q] = total[pl.ds((2 * q + parity) * slab, slab), :]
        send_ref[q] = total[pl.ds((2 * q + 1 - parity) * slab, slab), :].astype(BF16)


def finish(meta, parity, energy, factors, sets, density, integrals, narrow_count):
    lmo_dev, orbitals, auxiliary = density.shape
    steps = lmo_dev // 2
    static, parts = set_shapes(sets, steps)
    slab = auxiliary // narrow_count
    out = (narrow_count // 2, slab, auxiliary)
    buffers, sem = set_scratch(static, auxiliary)
    any_spec = pl.BlockSpec(memory_space=pl.ANY)
    vmem_spec = pl.BlockSpec(memory_space=pltpu.VMEM)
    smem_spec = pl.BlockSpec(memory_space=pltpu.SMEM)
    return pl.pallas_call(
        functools.partial(finish_kernel, static, steps, slab),
        out_shape=[
            pltpu.VMEM(out, F32),
            pltpu.VMEM(out, BF16),
            pltpu.VMEM(density.shape, F32),
        ],
        in_specs=[smem_spec, smem_spec, vmem_spec, vmem_spec]
        + [any_spec] * len(parts)
        + [vmem_spec, any_spec],
        out_specs=[vmem_spec] * 3,
        scratch_shapes=buffers
        + [
            pltpu.VMEM(integrals.shape, BF16),
            pltpu.VMEM((auxiliary, auxiliary), F32),
            sem,
            pltpu.SemaphoreType.DMA((lmo_dev,)),
        ],
        input_output_aliases={4 + len(parts): 2},
        cost_estimate=pl.CostEstimate(
            flops=2 * lmo_dev * orbitals * auxiliary * auxiliary,
            transcendentals=0,
            bytes_accessed=6 * density.size,
        ),
        compiler_params=pltpu.CompilerParams(vmem_limit_bytes=VMEM_LIMIT),
        name="finish",
    )(meta, parity, energy, factors, *parts, density, integrals)[:2]


def halve(x, axis, bit, high):
    pairs = x.reshape((x.shape[0] // 2, 2) + x.shape[1:])
    keep = jnp.where(high, pairs[:, 1], pairs[:, 0])
    send = jnp.where(high, pairs[:, 0], pairs[:, 1]).astype(BF16)
    return keep + xor_permute(send, axis, bit).astype(F32)


def bits_of(count):
    return [1 << b for b in range(count.bit_length() - 1)]


def local(factors, integrals, pao_energy, lmo_energy, partners):
    wide_count = lax.axis_size("wide")
    narrow_count = lax.axis_size("narrow")
    wide_index = lax.axis_index("wide")
    narrow_index = lax.axis_index("narrow")
    lmo_dev, orbitals, auxiliary = factors.shape
    pair_count = lmo_dev * PARTNERS
    group_pairs = lmo_dev // 2
    half = wide_count // 2
    chunk = orbitals * 5 // 16 // 16 * 16
    direct = 2 * chunk

    leading = factors[:, :chunk]
    leading, others = lax.optimization_barrier((leading, factors))
    mirrored = [xor_permute(x, "wide", half) for x in [leading, others[:, chunk:direct]]]

    column = lax.dynamic_index_in_dim(
        partners.reshape(wide_count, narrow_count, pair_count), narrow_index, 1, keepdims=False
    )
    groups = column // lmo_dev // narrow_count
    slots = column % lmo_dev
    ids = jnp.arange(wide_count, dtype=jnp.int32)
    hit = groups[:, :, None] == ids
    low = jnp.min(jnp.where(hit, slots[:, :, None], lmo_dev - 1), axis=1)
    high = jnp.max(jnp.where(hit, slots[:, :, None], 0), axis=1)
    asked = jnp.stack([low, high], axis=-1)
    order = wide_index ^ ids
    by_order = (order[:, None] == ids)[:, :, None]

    def asked_of(group):
        listed = lax.dynamic_index_in_dim(asked, group, 1, keepdims=False)
        return jnp.sum(jnp.where(by_order, listed[None], 0), axis=1, dtype=jnp.int32)

    asked = jnp.stack([asked_of(wide_index), asked_of(wide_index ^ half)]).reshape(-1)

    near = [
        xor_permute(x, "wide", d + 1)
        for d, x in enumerate(take_pairs(factors, asked, 2, half - 1, 0, orbitals))
    ]
    far_asked, mirrored[0] = lax.optimization_barrier((asked, mirrored[0]))
    far_rows = list(take_pairs(factors, far_asked, 2 * half, half, direct, orbitals - direct))
    late = half // 2
    forwarded = [
        [
            xor_permute(x, "wide", d + 1)
            for d, x in enumerate(take_pairs(m, asked, 2 * wide_count + 2, half - 1, 0, chunk))
        ]
        for m in mirrored
    ]

    far = []
    for d, x in enumerate(far_rows):
        if d >= late:
            x, far[d - late] = lax.optimization_barrier((x, far[d - late]))
        far.append(xor_permute(x, "wide", half + d))

    own_groups = lax.dynamic_index_in_dim(groups, wide_index, 0, keepdims=False)
    own_slots = lax.dynamic_index_in_dim(slots, wide_index, 0, keepdims=False)
    listed = lax.dynamic_index_in_dim(column, wide_index, 0, keepdims=False)
    own_low = lax.dynamic_index_in_dim(low, wide_index, 0, keepdims=False)
    own_high = lax.dynamic_index_in_dim(high, wide_index, 0, keepdims=False)
    pair_ids = jnp.arange(pair_count, dtype=jnp.int32)
    place = jnp.sum(
        (own_groups[:, None] == own_groups[None, :]) & (pair_ids[None, :] < pair_ids[:, None]),
        axis=1, dtype=jnp.int32,
    )
    steps = jnp.arange(group_pairs, dtype=jnp.int32)
    picked = (own_groups == order[:, None, None]) & (place == steps[None, :, None])

    def of_pair(values):
        return jnp.sum(jnp.where(picked, values, 0), axis=2, dtype=jnp.int32)

    valid = of_pair(jnp.ones_like(pair_ids))
    lmo = jnp.where(valid > 0, of_pair(pair_ids // PARTNERS), steps)
    lowest = jnp.sum(jnp.where(own_groups[:, None] == ids, own_low, 0), axis=1, dtype=jnp.int32)
    rank = of_pair((own_slots > lowest).astype(jnp.int32))
    bounds = jnp.stack([own_low, own_high], axis=-1)
    bounds = jnp.sum(jnp.where(by_order, bounds[None], 0), axis=1, dtype=jnp.int32)
    triples = jnp.stack([valid, lmo, rank], axis=-1).reshape(wide_count, 3 * group_pairs)
    meta = jnp.concatenate([bounds, triples], axis=1).reshape(-1)

    shifted = pao_energy - lmo_energy[:, None]
    first_lmo = (wide_index * narrow_count + narrow_index) * lmo_dev
    rows = jnp.concatenate([first_lmo + lmo, of_pair(listed)], axis=1)
    rows = jnp.pad(rows, ((0, 0), (0, -rows.shape[1] % 8)))
    energy = shifted.at[rows].get(mode="promise_in_bounds")

    highs = {("narrow", bit): (narrow_index & bit) > 0 for bit in bits_of(narrow_count)}
    highs |= {("wide", bit): (wide_index & bit) > 0 for bit in bits_of(wide_count)}
    parity = (narrow_index & 1).astype(jnp.int32).reshape(1)
    meta, parity, energy, highs = lax.optimization_barrier((meta, parity, energy, highs))

    def add(sets, density):
        return pair_terms(meta, energy, factors, sets, density)

    def far_set(d, begin, with_direct):
        parts = list(mirrored) if d == 0 else [pieces[d - 1] for pieces in forwarded]
        parts = parts[begin:] + [far[d]] if with_direct else parts[begin:1]
        return half + d, parts, begin * chunk

    density = add([(0, [factors], 0), (1, [near[0]], 0)], None)
    density = add([(d, [near[d - 1]], 0) for d in range(2, half)], density)
    density = add([far_set(d, 0, True) for d in range(late)], density)
    density = add([far_set(d, 0, False) for d in range(late, half)], density)

    keep, send = finish(
        meta, parity, energy, factors,
        [far_set(d, 1, True) for d in range(late, half)], density, integrals, narrow_count,
    )

    x = keep + xor_permute(send, "narrow", 1).astype(F32)
    for bit in bits_of(narrow_count)[1:]:
        x = halve(x, "narrow", bit, highs["narrow", bit])
    tile = (auxiliary // wide_count, auxiliary // narrow_count)
    x = x[0].T.reshape(wide_count, tile[0] * tile[1] // 128, 128)
    for bit in bits_of(wide_count):
        x = halve(x, "wide", bit, highs["wide", bit])
    return x[0].reshape(tile)


def solution(mesh):
    in_specs = (P(("wide", "narrow"), None, None), P(("wide", "narrow"), None, None), P(), P(), P())
    return jax.shard_map(
        local, mesh=mesh, in_specs=in_specs, out_specs=P("wide", "narrow"), check_vma=False
    )
```

```python
import functools

import jax
import jax.numpy as jnp
from jax import lax
from jax.experimental import pallas as pl
from jax.experimental.pallas import tpu as pltpu
from jax.sharding import PartitionSpec as P


PARTNERS = 4
F32 = jnp.float32
BF16 = jnp.bfloat16
VMEM_LIMIT = 24 << 20
MIRRORED_ROWS = (64, 144)


def xor_permute(x, axis, bit):
    return lax.ppermute(x, axis, [(i, i ^ bit) for i in range(lax.axis_size(axis))])


def take_kernel(base, rows, index_ref, source_ref, *refs):
    outputs, (buffer, loaded, stored) = refs[:-3], refs[-3:]
    first, count = rows
    loads, stores = [], []
    for k in range(2 * len(outputs)):
        lmo = source_ref.at[index_ref[base + k], pl.ds(first, count), :]
        loads.append(pltpu.make_async_copy(lmo, buffer.at[k], loaded.at[k]))
        target = outputs[k // 2].at[k % 2]
        stores.append(pltpu.make_async_copy(buffer.at[k], target, stored.at[k]))
    for load in loads:
        load.start()
    for load, store in zip(loads, stores):
        load.wait()
        store.start()
    for store in stores:
        store.wait()


def take_pairs(source, index, base, outputs, first, count):
    auxiliary = source.shape[2]
    any_spec = pl.BlockSpec(memory_space=pl.ANY)
    return pl.pallas_call(
        functools.partial(take_kernel, base, (first, count)),
        out_shape=[jax.ShapeDtypeStruct((2, count, auxiliary), source.dtype)] * outputs,
        grid_spec=pltpu.PrefetchScalarGridSpec(
            num_scalar_prefetch=1,
            grid=(1,),
            in_specs=[pl.BlockSpec(memory_space=pltpu.HBM)],
            out_specs=[any_spec] * outputs,
            scratch_shapes=[
                pltpu.VMEM((2 * outputs, count, auxiliary), source.dtype),
                pltpu.SemaphoreType.DMA((2 * outputs,)),
                pltpu.SemaphoreType.DMA((2 * outputs,)),
            ],
        ),
        cost_estimate=pl.CostEstimate(
            flops=0, transcendentals=0, bytes_accessed=8 * outputs * count * auxiliary
        ),
        compiler_params=pltpu.CompilerParams(vmem_limit_bytes=VMEM_LIMIT),
        name="take_pairs",
    )(index, source)


def start_all(copies):
    for copy in copies:
        copy.start()


def load_sets(sets, meta_ref, part_refs, buffers, sem):
    copies, part_refs = [], iter(part_refs)
    for (base, _, _, counts), buffer in zip(sets, buffers):
        loads, row = [], 0
        for count in counts:
            part_ref = next(part_refs)
            for r in range(2):
                slot = r if part_ref.shape[0] == 2 else meta_ref[base + r]
                target = buffer.at[r, pl.ds(row, count), :]
                number = sum(len(c) for c in copies) + len(loads)
                loads.append(pltpu.make_async_copy(part_ref.at[slot], target, sem.at[number]))
            row += count
        copies.append(loads)
    return copies


def add_sets(sets, copies, buffers, steps, meta_ref, energy_ref, factors_ref, density_ref):
    for (base, group, first, counts), loads, buffer in zip(sets, copies, buffers):
        for copy in loads:
            copy.wait()
        for k in range(steps):

            @pl.when(meta_ref[base + 2 + 3 * k] > 0)
            def _():
                lmo, rank = meta_ref[base + 3 + 3 * k], meta_ref[base + 4 + 3 * k]
                energy = energy_ref[group]
                own_energy = jnp.broadcast_to(energy[k : k + 1], (8, energy.shape[1])).T[:, :1]
                other = energy[steps + k : steps + k + 1, first : first + sum(counts)]
                part = buffer[rank]
                integral = lax.dot_general(
                    factors_ref[lmo], part, (((1,), (1,)), ((), ())), preferred_element_type=F32
                )
                amplitude = (integral / (own_energy + other)).astype(BF16)
                density_ref[lmo] += jnp.dot(amplitude, part, preferred_element_type=F32)


def pair_kernel(sets, steps, initial, meta_ref, energy_ref, factors_ref, *refs):
    count = sum(len(counts) for *_, counts in sets)
    part_refs, refs = refs[:count], refs[count if initial else count + 1 :]
    density_ref, buffers, sem = refs[0], refs[1:-1], refs[-1]
    copies = load_sets(sets, meta_ref, part_refs, buffers, sem)
    for loads in copies:
        start_all(loads)
    if initial:
        density_ref[...] = jnp.zeros_like(density_ref)
    add_sets(sets, copies, buffers, steps, meta_ref, energy_ref, factors_ref, density_ref)


def set_shapes(sets, steps):
    static = tuple(
        ((2 + 3 * steps) * group, group, first, tuple(part.shape[1] for part in parts))
        for group, parts, first in sets
    )
    return static, [part for _, parts, _ in sets for part in parts]


def set_scratch(static, auxiliary):
    count = sum(2 * len(counts) for *_, counts in static)
    return [
        pltpu.VMEM((2, sum(counts), auxiliary), BF16) for *_, counts in static
    ], pltpu.SemaphoreType.DMA((count,))


def pair_terms(meta, energy, factors, sets, density):
    lmo_dev, orbitals, auxiliary = factors.shape
    steps = lmo_dev // 2
    static, parts = set_shapes(sets, steps)
    initial = density is None
    buffers, sem = set_scratch(static, auxiliary)
    any_spec = pl.BlockSpec(memory_space=pl.ANY)
    vmem_spec = pl.BlockSpec(memory_space=pltpu.VMEM)
    return pl.pallas_call(
        functools.partial(pair_kernel, static, steps, initial),
        out_shape=pltpu.VMEM((lmo_dev, orbitals, auxiliary), F32),
        in_specs=[pl.BlockSpec(memory_space=pltpu.SMEM), vmem_spec, vmem_spec]
        + [any_spec] * len(parts)
        + ([] if initial else [vmem_spec]),
        out_specs=vmem_spec,
        scratch_shapes=buffers + [sem],
        input_output_aliases={} if initial else {3 + len(parts): 0},
        cost_estimate=pl.CostEstimate(
            flops=4 * len(sets) * steps * orbitals * orbitals * auxiliary,
            transcendentals=len(sets) * steps * orbitals * orbitals,
            bytes_accessed=4 * len(sets) * orbitals * auxiliary,
        ),
        compiler_params=pltpu.CompilerParams(vmem_limit_bytes=VMEM_LIMIT),
        name="pair_terms",
    )(meta, energy, factors, *parts, *([] if initial else [density]))


def dense_tiles(total, first, wide_count):
    rows = total.shape[0] // wide_count
    whole_even, middle, whole_odd = [
        total[:, first + 128 * j : first + 128 * (j + 1)].reshape(wide_count, rows, 128)
        for j in range(3)
    ]
    upper, lower = middle[:, : rows // 2], middle[:, rows // 2 :]
    left = lax.broadcasted_iota(jnp.int32, upper.shape, 2) < 64
    half_even = jnp.where(left, upper, pltpu.roll(lower, 64, axis=2))
    half_odd = jnp.where(left, pltpu.roll(upper, 64, axis=2), lower)
    return (
        jnp.concatenate([whole_even, half_even], axis=1),
        jnp.concatenate([whole_odd, half_odd], axis=1),
    )


def sparse_tile(dense, odd):
    rows = dense.shape[0] * 2 // 3
    whole = dense[:rows]
    half = jnp.concatenate([dense[rows:, :64], dense[rows:, 64:]], axis=0)
    return jnp.where(
        odd, jnp.concatenate([half, whole], axis=1), jnp.concatenate([whole, half], axis=1)
    )


def finish_kernel(sets, steps, slab, meta_ref, parity_ref, energy_ref, factors_ref, *refs):
    count = sum(len(counts) for *_, counts in sets)
    part_refs, refs = refs[:count], refs[count:]
    _, integrals_ref, keep_ref, send_ref, density_ref = refs[:5]
    buffers, (total, sem) = refs[5:-2], refs[-2:]
    copies = load_sets(sets, meta_ref, part_refs, buffers, sem)
    for group in copies:
        start_all(group)
    add_sets(sets, copies, buffers, steps, meta_ref, energy_ref, factors_ref, density_ref)
    for i in range(density_ref.shape[0]):
        term = lax.dot_general(
            integrals_ref[i], density_ref[i].astype(BF16), (((0,), (0,)), ((), ())),
            preferred_element_type=F32,
        )
        if i == 0:
            total[...] = term
        else:
            total[...] += term
    value = total[...]
    total[...] = 0.5 * (value + value.T)
    parity = parity_ref[0]
    for q in range(keep_ref.shape[0]):
        if keep_ref.ndim == 3:
            keep_ref[q] = total[pl.ds((2 * q + parity) * slab, slab), :]
            send_ref[q] = total[pl.ds((2 * q + 1 - parity) * slab, slab), :].astype(BF16)
            continue
        even, odd = dense_tiles(total, 2 * q * slab, keep_ref.shape[1])

        @pl.when(parity == 0)
        def _():
            keep_ref[q] = even
            send_ref[q] = odd.astype(BF16)

        @pl.when(parity == 1)
        def _():
            keep_ref[q] = odd
            send_ref[q] = even.astype(BF16)


def finish(meta, parity, energy, factors, sets, density, integrals, counts):
    lmo_dev, orbitals, auxiliary = density.shape
    steps = lmo_dev // 2
    static, parts = set_shapes(sets, steps)
    wide_count, narrow_count = counts
    slab, rows = auxiliary // narrow_count, auxiliary // wide_count
    out = (narrow_count // 2, slab, auxiliary)
    if slab == 192 and rows % 32 == 0:
        out = (narrow_count // 2, wide_count, rows * slab // 128, 128)
    buffers, sem = set_scratch(static, auxiliary)
    vmem_spec = pl.BlockSpec(memory_space=pltpu.VMEM)
    smem_spec = pl.BlockSpec(memory_space=pltpu.SMEM)
    return pl.pallas_call(
        functools.partial(finish_kernel, static, steps, slab),
        out_shape=[
            pltpu.VMEM(out, F32),
            pltpu.VMEM(out, BF16),
            pltpu.VMEM(density.shape, F32),
        ],
        in_specs=[smem_spec, smem_spec, vmem_spec, vmem_spec]
        + [vmem_spec] * len(parts)
        + [vmem_spec, vmem_spec],
        out_specs=[vmem_spec] * 3,
        scratch_shapes=buffers + [pltpu.VMEM((auxiliary, auxiliary), F32), sem],
        input_output_aliases={4 + len(parts): 2},
        cost_estimate=pl.CostEstimate(
            flops=2 * lmo_dev * orbitals * auxiliary * auxiliary,
            transcendentals=0,
            bytes_accessed=6 * density.size,
        ),
        compiler_params=pltpu.CompilerParams(vmem_limit_bytes=VMEM_LIMIT),
        name="finish",
    )(meta, parity, energy, factors, *parts, density, integrals)[:2]


def halve(x, axis, bit, high, dim):
    pairs = x.reshape(x.shape[:dim] + (x.shape[dim] // 2, 2) + x.shape[dim + 1 :])
    first, second = [lax.index_in_dim(pairs, b, dim + 1, keepdims=False) for b in range(2)]
    keep = jnp.where(high, second, first)
    send = jnp.where(high, first, second).astype(BF16)
    return keep + xor_permute(send, axis, bit).astype(F32)


def bits_of(count):
    return [1 << b for b in range(count.bit_length() - 1)]


def local(factors, integrals, pao_energy, lmo_energy, partners):
    wide_count = lax.axis_size("wide")
    narrow_count = lax.axis_size("narrow")
    wide_index = lax.axis_index("wide")
    narrow_index = lax.axis_index("narrow")
    lmo_dev, orbitals, auxiliary = factors.shape
    pair_count = lmo_dev * PARTNERS
    group_pairs = lmo_dev // 2
    half = wide_count // 2
    chunk, direct = [orbitals * c // 256 // 16 * 16 for c in MIRRORED_ROWS]

    leading = factors[:, :chunk]
    leading, others = lax.optimization_barrier((leading, factors))
    mirrored = [xor_permute(x, "wide", half) for x in [leading, others[:, chunk:direct]]]

    column = lax.dynamic_index_in_dim(
        partners.reshape(wide_count, narrow_count, pair_count), narrow_index, 1, keepdims=False
    )
    groups = column // lmo_dev // narrow_count
    slots = column % lmo_dev
    ids = jnp.arange(wide_count, dtype=jnp.int32)
    hit = groups[:, :, None] == ids
    low = jnp.min(jnp.where(hit, slots[:, :, None], lmo_dev - 1), axis=1)
    high = jnp.max(jnp.where(hit, slots[:, :, None], 0), axis=1)
    asked = jnp.stack([low, high], axis=-1)
    order = wide_index ^ ids
    by_order = (order[:, None] == ids)[:, :, None]

    def asked_of(group):
        listed = lax.dynamic_index_in_dim(asked, group, 1, keepdims=False)
        return jnp.sum(jnp.where(by_order, listed[None], 0), axis=1, dtype=jnp.int32)

    asked = jnp.stack([asked_of(wide_index), asked_of(wide_index ^ half)]).reshape(-1)

    near = [
        xor_permute(x, "wide", d + 1)
        for d, x in enumerate(take_pairs(factors, asked, 2, half - 1, 0, orbitals))
    ]
    far_asked, mirrored[0] = lax.optimization_barrier((asked, mirrored[0]))
    far_rows = list(take_pairs(factors, far_asked, 2 * half, half, direct, orbitals - direct))
    late = half // 2
    forwarded = [
        [
            xor_permute(x, "wide", d + 1)
            for d, x in enumerate(take_pairs(m, asked, 2 * wide_count + 2, half - 1, 0, m.shape[1]))
        ]
        for m in mirrored
    ]

    far = [xor_permute(x, "wide", half + d) for d, x in enumerate(far_rows)]

    own_groups = lax.dynamic_index_in_dim(groups, wide_index, 0, keepdims=False)
    own_slots = lax.dynamic_index_in_dim(slots, wide_index, 0, keepdims=False)
    listed = lax.dynamic_index_in_dim(column, wide_index, 0, keepdims=False)
    own_low = lax.dynamic_index_in_dim(low, wide_index, 0, keepdims=False)
    own_high = lax.dynamic_index_in_dim(high, wide_index, 0, keepdims=False)
    pair_ids = jnp.arange(pair_count, dtype=jnp.int32)
    place = jnp.sum(
        (own_groups[:, None] == own_groups[None, :]) & (pair_ids[None, :] < pair_ids[:, None]),
        axis=1, dtype=jnp.int32,
    )
    steps = jnp.arange(group_pairs, dtype=jnp.int32)
    picked = (own_groups == order[:, None, None]) & (place == steps[None, :, None])

    def of_pair(values):
        return jnp.sum(jnp.where(picked, values, 0), axis=2, dtype=jnp.int32)

    valid = of_pair(jnp.ones_like(pair_ids))
    lmo = jnp.where(valid > 0, of_pair(pair_ids // PARTNERS), steps)
    lowest = jnp.sum(jnp.where(own_groups[:, None] == ids, own_low, 0), axis=1, dtype=jnp.int32)
    rank = of_pair((own_slots > lowest).astype(jnp.int32))
    bounds = jnp.stack([own_low, own_high], axis=-1)
    bounds = jnp.sum(jnp.where(by_order, bounds[None], 0), axis=1, dtype=jnp.int32)
    triples = jnp.stack([valid, lmo, rank], axis=-1).reshape(wide_count, 3 * group_pairs)
    meta = jnp.concatenate([bounds, triples], axis=1).reshape(-1)

    shifted = pao_energy - lmo_energy[:, None]
    first_lmo = (wide_index * narrow_count + narrow_index) * lmo_dev
    rows = jnp.concatenate([first_lmo + lmo, of_pair(listed)], axis=1)
    rows = jnp.pad(rows, ((0, 0), (0, -rows.shape[1] % 8)))
    energy = shifted.at[rows].get(mode="promise_in_bounds")

    highs = {("narrow", bit): (narrow_index & bit) > 0 for bit in bits_of(narrow_count)}
    highs |= {("wide", bit): (wide_index & bit) > 0 for bit in bits_of(wide_count)}
    parity = (narrow_index & 1).astype(jnp.int32).reshape(1)
    meta, parity, energy, highs = lax.optimization_barrier((meta, parity, energy, highs))

    def add(sets, density):
        return pair_terms(meta, energy, factors, sets, density)

    def far_set(d, begin=0, end=3):
        parts = list(mirrored) if d == 0 else [pieces[d - 1] for pieces in forwarded]
        return half + d, (parts + [far[d]])[begin:end], begin * chunk

    density = add([(0, [factors], 0), (1, [near[0]], 0)], None)
    density = add([(d, [near[d - 1]], 0) for d in range(2, half)], density)
    density = add([far_set(half - 1, 0, 1)], density)
    density = add([far_set(d) for d in range(late)], density)
    density = add([far_set(d) for d in range(late, half - 1)], density)
    keep, send = finish(
        meta, parity, energy, factors,
        [far_set(half - 1, 1)], density, integrals,
        (wide_count, narrow_count),
    )

    x = keep + xor_permute(send, "narrow", 1).astype(F32)
    tile = (auxiliary // wide_count, auxiliary // narrow_count)
    packed = x.ndim == 4
    if not packed:
        x = x.transpose(0, 2, 1)
    x = x.reshape(narrow_count // 2, 2, half, tile[0] * tile[1] // 128, 128)
    y_bits = [("narrow", bit) for bit in bits_of(narrow_count)[1:]]
    x_bits = [("wide", bit) for bit in bits_of(wide_count)[: len(y_bits)]]
    paths = [x[:, 0], x[:, 1]]
    for step in range(2 * len(y_bits)):
        for p, order in enumerate([y_bits + x_bits, x_bits + y_bits]):
            axis, bit = order[step]
            paths[p] = halve(paths[p], axis, bit, highs[axis, bit], 0 if axis == "narrow" else 1)
    x = jnp.concatenate(paths, axis=1)[0]
    for bit in bits_of(wide_count)[len(y_bits) :]:
        x = halve(x, "wide", bit, highs["wide", bit], 0)
    return sparse_tile(x[0], highs["narrow", 1]) if packed else x[0].reshape(tile)


def solution(mesh):
    in_specs = (P(("wide", "narrow"), None, None), P(("wide", "narrow"), None, None), P(), P(), P())
    return jax.shard_map(
        local, mesh=mesh, in_specs=in_specs, out_specs=P("wide", "narrow"), check_vma=False
    )
```

```python
import functools

import jax
import jax.numpy as jnp
from jax import lax
from jax.experimental import pallas as pl
from jax.experimental.pallas import tpu as pltpu
from jax.sharding import PartitionSpec as P


PARTNERS = 4
F32 = jnp.float32
BF16 = jnp.bfloat16
VMEM_LIMIT = 24 << 20
MIRRORED_ROWS = (64, 144)


def xor_permute(x, axis, bit):
    return lax.ppermute(x, axis, [(i, i ^ bit) for i in range(lax.axis_size(axis))])


def take_kernel(base, rows, index_ref, source_ref, *refs):
    outputs, sem = refs[:-1], refs[-1]
    first, count = rows
    copies = []
    for k in range(2 * len(outputs)):
        lmo = source_ref.at[index_ref[base + k], pl.ds(first, count), :]
        copies.append(pltpu.make_async_copy(lmo, outputs[k // 2].at[k % 2], sem.at[k]))
    start_all(copies)
    for copy in copies:
        copy.wait()


def take_pairs(source, index, base, outputs, first, count, limit=VMEM_LIMIT):
    auxiliary = source.shape[2]
    return pl.pallas_call(
        functools.partial(take_kernel, base, (first, count)),
        out_shape=[pltpu.VMEM((2, count, auxiliary), source.dtype)] * outputs,
        in_specs=[
            pl.BlockSpec(memory_space=pltpu.SMEM),
            pl.BlockSpec(memory_space=pl.ANY),
        ],
        out_specs=[pl.BlockSpec(memory_space=pltpu.VMEM)] * outputs,
        scratch_shapes=[pltpu.SemaphoreType.DMA((2 * outputs,))],
        cost_estimate=pl.CostEstimate(
            flops=0, transcendentals=0, bytes_accessed=8 * outputs * count * auxiliary
        ),
        compiler_params=pltpu.CompilerParams(vmem_limit_bytes=limit),
        name="take_pairs",
    )(index, source)


def start_all(copies):
    for copy in copies:
        copy.start()


def load_sets(sets, meta_ref, part_refs, buffers, sem):
    copies, part_refs = [], iter(part_refs)
    for (base, _, _, counts), buffer in zip(sets, buffers):
        loads, row = [], 0
        for count in counts:
            part_ref = next(part_refs)
            for r in range(2):
                slot = r if part_ref.shape[0] == 2 else meta_ref[base + r]
                target = buffer.at[r, pl.ds(row, count), :]
                number = sum(len(c) for c in copies) + len(loads)
                loads.append(pltpu.make_async_copy(part_ref.at[slot], target, sem.at[number]))
            row += count
        copies.append(loads)
    return copies


def add_sets(sets, copies, buffers, steps, meta_ref, energy_ref, factors_ref, density_ref):
    for (base, group, first, counts), loads, buffer in zip(sets, copies, buffers):
        for copy in loads:
            copy.wait()
        for k in range(steps):

            @pl.when(meta_ref[base + 2 + 3 * k] > 0)
            def _():
                lmo, rank = meta_ref[base + 3 + 3 * k], meta_ref[base + 4 + 3 * k]
                energy = energy_ref[group]
                own_energy = jnp.broadcast_to(energy[k : k + 1], (8, energy.shape[1])).T[:, :1]
                other = energy[steps + k : steps + k + 1, first : first + sum(counts)]
                part = buffer[rank]
                integral = lax.dot_general(
                    factors_ref[lmo], part, (((1,), (1,)), ((), ())), preferred_element_type=F32
                )
                amplitude = (integral / (own_energy + other)).astype(BF16)
                density_ref[lmo] += jnp.dot(amplitude, part, preferred_element_type=F32)


def pair_kernel(sets, steps, initial, meta_ref, energy_ref, factors_ref, *refs):
    count = sum(len(counts) for *_, counts in sets)
    part_refs, refs = refs[:count], refs[count if initial else count + 1 :]
    density_ref, buffers, sem = refs[0], refs[1:-1], refs[-1]
    copies = load_sets(sets, meta_ref, part_refs, buffers, sem)
    for loads in copies:
        start_all(loads)
    if initial:
        density_ref[...] = jnp.zeros_like(density_ref)
    add_sets(sets, copies, buffers, steps, meta_ref, energy_ref, factors_ref, density_ref)


def set_shapes(sets, steps):
    static = tuple(
        ((2 + 3 * steps) * group, group, first, tuple(part.shape[1] for part in parts))
        for group, parts, first in sets
    )
    return static, [part for _, parts, _ in sets for part in parts]


def set_scratch(static, auxiliary):
    count = sum(2 * len(counts) for *_, counts in static)
    return [
        pltpu.VMEM((2, sum(counts), auxiliary), BF16) for *_, counts in static
    ], pltpu.SemaphoreType.DMA((count,))


def pair_terms(meta, energy, factors, sets, density):
    lmo_dev, orbitals, auxiliary = factors.shape
    steps = lmo_dev // 2
    static, parts = set_shapes(sets, steps)
    initial = density is None
    buffers, sem = set_scratch(static, auxiliary)
    any_spec = pl.BlockSpec(memory_space=pl.ANY)
    vmem_spec = pl.BlockSpec(memory_space=pltpu.VMEM)
    return pl.pallas_call(
        functools.partial(pair_kernel, static, steps, initial),
        out_shape=pltpu.VMEM((lmo_dev, orbitals, auxiliary), F32),
        in_specs=[pl.BlockSpec(memory_space=pltpu.SMEM), vmem_spec, vmem_spec]
        + [any_spec] * len(parts)
        + ([] if initial else [vmem_spec]),
        out_specs=vmem_spec,
        scratch_shapes=buffers + [sem],
        input_output_aliases={} if initial else {3 + len(parts): 0},
        cost_estimate=pl.CostEstimate(
            flops=4 * len(sets) * steps * orbitals * orbitals * auxiliary,
            transcendentals=len(sets) * steps * orbitals * orbitals,
            bytes_accessed=4 * len(sets) * orbitals * auxiliary,
        ),
        compiler_params=pltpu.CompilerParams(vmem_limit_bytes=VMEM_LIMIT),
        name="pair_terms",
    )(meta, energy, factors, *parts, *([] if initial else [density]))


def is_last_lmo(base, steps, meta_ref, lmo):
    return functools.reduce(
        jnp.logical_or, [meta_ref[base + 3 + 3 * k] == lmo for k in range(steps)]
    )


def add_total(total, integral, density):
    total[...] += lax.dot_general(
        integral, density.astype(BF16), (((0,), (0,)), ((), ())), preferred_element_type=F32
    )


def partial_kernel(base, steps, meta_ref, integrals_ref, density_ref, total_ref):
    total_ref[...] = jnp.zeros_like(total_ref)
    for i in range(density_ref.shape[0]):

        @pl.when(jnp.logical_not(is_last_lmo(base, steps, meta_ref, i)))
        def _():
            add_total(total_ref, integrals_ref[i], density_ref[i])


def partial_total(meta, group, density, integrals):
    lmo_dev, orbitals, auxiliary = density.shape
    steps = lmo_dev // 2
    vmem_spec = pl.BlockSpec(memory_space=pltpu.VMEM)
    return pl.pallas_call(
        functools.partial(partial_kernel, (2 + 3 * steps) * group, steps),
        out_shape=pltpu.VMEM((auxiliary, auxiliary), F32),
        in_specs=[pl.BlockSpec(memory_space=pltpu.SMEM), vmem_spec, vmem_spec],
        out_specs=vmem_spec,
        cost_estimate=pl.CostEstimate(
            flops=lmo_dev * orbitals * auxiliary * auxiliary,
            transcendentals=0,
            bytes_accessed=integrals.size,
        ),
        compiler_params=pltpu.CompilerParams(vmem_limit_bytes=VMEM_LIMIT),
        name="partial_total",
    )(meta, integrals, density)


def dense_tiles(total, first, wide_count):
    rows = total.shape[0] // wide_count
    whole_even, middle, whole_odd = [
        total[:, first + 128 * j : first + 128 * (j + 1)].reshape(wide_count, rows, 128)
        for j in range(3)
    ]
    upper, lower = middle[:, : rows // 2], middle[:, rows // 2 :]
    left = lax.broadcasted_iota(jnp.int32, upper.shape, 2) < 64
    half_even = jnp.where(left, upper, pltpu.roll(lower, 64, axis=2))
    half_odd = jnp.where(left, pltpu.roll(upper, 64, axis=2), lower)
    return (
        jnp.concatenate([whole_even, half_even], axis=1),
        jnp.concatenate([whole_odd, half_odd], axis=1),
    )


def sparse_tile(dense, odd):
    rows = dense.shape[0] * 2 // 3
    whole = dense[:rows]
    half = jnp.concatenate([dense[rows:, :64], dense[rows:, 64:]], axis=0)
    return jnp.where(
        odd, jnp.concatenate([half, whole], axis=1), jnp.concatenate([whole, half], axis=1)
    )


def finish_kernel(sets, steps, slab, meta_ref, parity_ref, energy_ref, factors_ref, *refs):
    count = sum(len(counts) for *_, counts in sets)
    part_refs, refs = refs[:count], refs[count:]
    _, integrals_ref, _, keep_ref, send_ref, density_ref, total = refs[:7]
    buffers, sem = refs[7:-1], refs[-1]
    copies = load_sets(sets, meta_ref, part_refs, buffers, sem)
    for group in copies:
        start_all(group)
    add_sets(sets, copies, buffers, steps, meta_ref, energy_ref, factors_ref, density_ref)
    for k in range(steps):
        lmo = meta_ref[sets[0][0] + 3 + 3 * k]
        add_total(total, integrals_ref[lmo], density_ref[lmo])
    value = total[...]
    total[...] = 0.5 * (value + value.T)
    parity = parity_ref[0]
    for q in range(keep_ref.shape[0]):
        if keep_ref.ndim == 3:
            keep_ref[q] = total[pl.ds((2 * q + parity) * slab, slab), :]
            send_ref[q] = total[pl.ds((2 * q + 1 - parity) * slab, slab), :].astype(BF16)
            continue
        even, odd = dense_tiles(total, 2 * q * slab, keep_ref.shape[1])

        @pl.when(parity == 0)
        def _():
            keep_ref[q] = even
            send_ref[q] = odd.astype(BF16)

        @pl.when(parity == 1)
        def _():
            keep_ref[q] = odd
            send_ref[q] = even.astype(BF16)


def finish(meta, parity, energy, factors, sets, density, integrals, total, counts):
    lmo_dev, orbitals, auxiliary = density.shape
    steps = lmo_dev // 2
    static, parts = set_shapes(sets, steps)
    wide_count, narrow_count = counts
    slab, rows = auxiliary // narrow_count, auxiliary // wide_count
    out = (narrow_count // 2, slab, auxiliary)
    if slab == 192 and rows % 32 == 0:
        out = (narrow_count // 2, wide_count, rows * slab // 128, 128)
    buffers, sem = set_scratch(static, auxiliary)
    vmem_spec = pl.BlockSpec(memory_space=pltpu.VMEM)
    smem_spec = pl.BlockSpec(memory_space=pltpu.SMEM)
    return pl.pallas_call(
        functools.partial(finish_kernel, static, steps, slab),
        out_shape=[
            pltpu.VMEM(out, F32),
            pltpu.VMEM(out, BF16),
            pltpu.VMEM(density.shape, F32),
            pltpu.VMEM(total.shape, F32),
        ],
        in_specs=[smem_spec, smem_spec, vmem_spec, vmem_spec]
        + [vmem_spec] * len(parts)
        + [vmem_spec] * 3,
        out_specs=[vmem_spec] * 4,
        scratch_shapes=buffers + [sem],
        input_output_aliases={4 + len(parts): 2, 6 + len(parts): 3},
        cost_estimate=pl.CostEstimate(
            flops=2 * lmo_dev * orbitals * auxiliary * auxiliary,
            transcendentals=0,
            bytes_accessed=6 * density.size,
        ),
        compiler_params=pltpu.CompilerParams(vmem_limit_bytes=VMEM_LIMIT),
        name="finish",
    )(meta, parity, energy, factors, *parts, density, integrals, total)[:2]


def halve(x, axis, bit, high, dim):
    pairs = x.reshape(x.shape[:dim] + (x.shape[dim] // 2, 2) + x.shape[dim + 1 :])
    first, second = [lax.index_in_dim(pairs, b, dim + 1, keepdims=False) for b in range(2)]
    keep = jnp.where(high, second, first)
    send = jnp.where(high, first, second).astype(BF16)
    return keep + xor_permute(send, axis, bit).astype(F32)


def bits_of(count):
    return [1 << b for b in range(count.bit_length() - 1)]


def local(factors, integrals, pao_energy, lmo_energy, partners):
    wide_count = lax.axis_size("wide")
    narrow_count = lax.axis_size("narrow")
    wide_index = lax.axis_index("wide")
    narrow_index = lax.axis_index("narrow")
    lmo_dev, orbitals, auxiliary = factors.shape
    pair_count = lmo_dev * PARTNERS
    group_pairs = lmo_dev // 2
    half = wide_count // 2
    chunk, direct = [orbitals * c // 256 // 16 * 16 for c in MIRRORED_ROWS]

    leading = factors[:, :chunk]
    leading, others = lax.optimization_barrier((leading, factors))
    mirrored = [xor_permute(x, "wide", half) for x in [leading, others[:, chunk:direct]]]

    column = lax.dynamic_index_in_dim(
        partners.reshape(wide_count, narrow_count, pair_count), narrow_index, 1, keepdims=False
    )
    groups = column // lmo_dev // narrow_count
    slots = column % lmo_dev
    ids = jnp.arange(wide_count, dtype=jnp.int32)
    hit = groups[:, :, None] == ids
    low = jnp.min(jnp.where(hit, slots[:, :, None], lmo_dev - 1), axis=1)
    high = jnp.max(jnp.where(hit, slots[:, :, None], 0), axis=1)
    asked = jnp.stack([low, high], axis=-1)
    order = wide_index ^ ids
    by_order = (order[:, None] == ids)[:, :, None]

    def asked_of(group):
        listed = lax.dynamic_index_in_dim(asked, group, 1, keepdims=False)
        return jnp.sum(jnp.where(by_order, listed[None], 0), axis=1, dtype=jnp.int32)

    asked = jnp.stack([asked_of(wide_index), asked_of(wide_index ^ half)]).reshape(-1)

    limit = (64 << 20) - (half - 1) * 4 * orbitals * auxiliary - (3 << 19)
    near = [
        xor_permute(x, "wide", d + 1)
        for d, x in enumerate(take_pairs(factors, asked, 2, half - 1, 0, orbitals, limit))
    ]
    far_asked, mirrored[0] = lax.optimization_barrier((asked, mirrored[0]))
    far_rows = list(take_pairs(factors, far_asked, 2 * half, half, direct, orbitals - direct))
    late = half // 2
    forwarded = [
        [
            xor_permute(x, "wide", d + 1)
            for d, x in enumerate(take_pairs(m, asked, 2 * wide_count + 2, half - 1, 0, m.shape[1]))
        ]
        for m in mirrored
    ]

    far = [xor_permute(x, "wide", half + d) for d, x in enumerate(far_rows)]

    own_groups = lax.dynamic_index_in_dim(groups, wide_index, 0, keepdims=False)
    own_slots = lax.dynamic_index_in_dim(slots, wide_index, 0, keepdims=False)
    listed = lax.dynamic_index_in_dim(column, wide_index, 0, keepdims=False)
    own_low = lax.dynamic_index_in_dim(low, wide_index, 0, keepdims=False)
    own_high = lax.dynamic_index_in_dim(high, wide_index, 0, keepdims=False)
    pair_ids = jnp.arange(pair_count, dtype=jnp.int32)
    place = jnp.sum(
        (own_groups[:, None] == own_groups[None, :]) & (pair_ids[None, :] < pair_ids[:, None]),
        axis=1, dtype=jnp.int32,
    )
    steps = jnp.arange(group_pairs, dtype=jnp.int32)
    picked = (own_groups == order[:, None, None]) & (place == steps[None, :, None])

    def of_pair(values):
        return jnp.sum(jnp.where(picked, values, 0), axis=2, dtype=jnp.int32)

    valid = of_pair(jnp.ones_like(pair_ids))
    lmo = jnp.where(valid > 0, of_pair(pair_ids // PARTNERS), steps)
    lowest = jnp.sum(jnp.where(own_groups[:, None] == ids, own_low, 0), axis=1, dtype=jnp.int32)
    rank = of_pair((own_slots > lowest).astype(jnp.int32))
    bounds = jnp.stack([own_low, own_high], axis=-1)
    bounds = jnp.sum(jnp.where(by_order, bounds[None], 0), axis=1, dtype=jnp.int32)
    triples = jnp.stack([valid, lmo, rank], axis=-1).reshape(wide_count, 3 * group_pairs)
    meta = jnp.concatenate([bounds, triples], axis=1).reshape(-1)

    shifted = pao_energy - lmo_energy[:, None]
    first_lmo = (wide_index * narrow_count + narrow_index) * lmo_dev
    rows = jnp.concatenate([first_lmo + lmo, of_pair(listed)], axis=1)
    rows = jnp.pad(rows, ((0, 0), (0, -rows.shape[1] % 8)))
    energy = shifted.at[rows].get(mode="promise_in_bounds")

    highs = {("narrow", bit): (narrow_index & bit) > 0 for bit in bits_of(narrow_count)}
    highs |= {("wide", bit): (wide_index & bit) > 0 for bit in bits_of(wide_count)}
    parity = (narrow_index & 1).astype(jnp.int32).reshape(1)
    meta, parity, energy, highs = lax.optimization_barrier((meta, parity, energy, highs))

    def add(sets, density):
        return pair_terms(meta, energy, factors, sets, density)

    def far_set(d):
        parts = list(mirrored) if d == 0 else [pieces[d - 1] for pieces in forwarded]
        return half + d, parts + [far[d]], 0

    density = add([(0, [factors], 0), (1, [near[0]], 0)], None)
    density = add([(d, [near[d - 1]], 0) for d in range(2, half)], density)
    density = add([far_set(d) for d in range(late)], density)
    density = add([far_set(d) for d in range(late, half - 1)], density)
    total = partial_total(meta, wide_count - 1, density, integrals)
    keep, send = finish(
        meta, parity, energy, factors,
        [far_set(half - 1)], density, integrals, total,
        (wide_count, narrow_count),
    )

    x = keep + xor_permute(send, "narrow", 1).astype(F32)
    tile = (auxiliary // wide_count, auxiliary // narrow_count)
    packed = x.ndim == 4
    if not packed:
        x = x.transpose(0, 2, 1)
    x = x.reshape(narrow_count // 2, 2, half, tile[0] * tile[1] // 128, 128)
    y_bits = [("narrow", bit) for bit in bits_of(narrow_count)[1:]]
    x_bits = [("wide", bit) for bit in bits_of(wide_count)[: len(y_bits)]]
    paths = [x[:, 0], x[:, 1]]
    for step in range(2 * len(y_bits)):
        for p, order in enumerate([y_bits + x_bits, x_bits + y_bits]):
            axis, bit = order[step]
            paths[p] = halve(paths[p], axis, bit, highs[axis, bit], 0 if axis == "narrow" else 1)
    x = jnp.concatenate(paths, axis=1)[0]
    for bit in bits_of(wide_count)[len(y_bits) :]:
        x = halve(x, "wide", bit, highs["wide", bit], 0)
    return sparse_tile(x[0], highs["narrow", 1]) if packed else x[0].reshape(tile)


def solution(mesh):
    in_specs = (P(("wide", "narrow"), None, None), P(("wide", "narrow"), None, None), P(), P(), P())
    return jax.shard_map(
        local, mesh=mesh, in_specs=in_specs, out_specs=P("wide", "narrow"), check_vma=False
    )
```

```python
import functools

import jax
import jax.numpy as jnp
from jax import lax
from jax.experimental import pallas as pl
from jax.experimental.pallas import tpu as pltpu
from jax.sharding import PartitionSpec as P


PARTNERS = 4
F32 = jnp.float32
BF16 = jnp.bfloat16
VMEM_LIMIT = 24 << 20
MIRRORED_ROWS = (64, 160)


def xor_permute(x, axis, bit):
    return lax.ppermute(x, axis, [(i, i ^ bit) for i in range(lax.axis_size(axis))])


def take_kernel(base, rows, index_ref, source_ref, *refs):
    outputs, sem = refs[:-1], refs[-1]
    first, count = rows
    copies = []
    for k in range(2 * len(outputs)):
        lmo = source_ref.at[index_ref[base + k], pl.ds(first, count), :]
        copies.append(pltpu.make_async_copy(lmo, outputs[k // 2].at[k % 2], sem.at[k]))
    start_all(copies)
    for copy in copies:
        copy.wait()


def take_near_kernel(offsets, lmo_dev, partners_ref, source_ref, *refs):
    outputs, (buffer, loaded, stored) = refs[:-3], refs[-3:]
    narrow_count = lax.axis_size("narrow")
    wide_index, narrow_index = lax.axis_index("wide"), lax.axis_index("narrow")
    first = (wide_index * narrow_count + narrow_index) * lmo_dev
    loads, stores = [], []
    for number, offset in enumerate(offsets):
        asker = ((wide_index ^ offset) * narrow_count + narrow_index) * lmo_dev
        low, high = jnp.int32(lmo_dev - 1), jnp.int32(0)
        for i in range(lmo_dev):
            for k in range(PARTNERS):
                slot = partners_ref[k, asker + i] - first
                hit = jnp.logical_and(slot >= 0, slot < lmo_dev)
                low = jnp.where(hit, jnp.minimum(low, slot), low)
                high = jnp.where(hit, jnp.maximum(high, slot), high)
        for r, slot in enumerate((low, high)):
            k = 2 * number + r
            loads.append(pltpu.make_async_copy(source_ref.at[slot], buffer.at[k], loaded.at[k]))
            stores.append(
                pltpu.make_async_copy(buffer.at[k], outputs[number].at[r], stored.at[k])
            )
            loads[-1].start()
    for load, store in zip(loads, stores):
        load.wait()
        store.start()
    for store in stores:
        store.wait()


def take_near(source, partners, offsets, limit):
    lmo_dev, orbitals, auxiliary = source.shape
    count = len(offsets)
    any_spec = pl.BlockSpec(memory_space=pl.ANY)
    return pl.pallas_call(
        functools.partial(take_near_kernel, offsets, lmo_dev),
        out_shape=[jax.ShapeDtypeStruct((2, orbitals, auxiliary), source.dtype)] * count,
        in_specs=[pl.BlockSpec(memory_space=pltpu.SMEM), any_spec],
        out_specs=[any_spec] * count,
        scratch_shapes=[
            pltpu.VMEM((2 * count, orbitals, auxiliary), source.dtype),
            pltpu.SemaphoreType.DMA((2 * count,)),
            pltpu.SemaphoreType.DMA((2 * count,)),
        ],
        cost_estimate=pl.CostEstimate(
            flops=0, transcendentals=0, bytes_accessed=8 * count * orbitals * auxiliary
        ),
        compiler_params=pltpu.CompilerParams(vmem_limit_bytes=limit),
        name="take_near",
    )(partners.T, source)


def take_pairs(source, index, base, outputs, first, count, limit=VMEM_LIMIT):
    auxiliary = source.shape[2]
    return pl.pallas_call(
        functools.partial(take_kernel, base, (first, count)),
        out_shape=[pltpu.VMEM((2, count, auxiliary), source.dtype)] * outputs,
        in_specs=[
            pl.BlockSpec(memory_space=pltpu.SMEM),
            pl.BlockSpec(memory_space=pl.ANY),
        ],
        out_specs=[pl.BlockSpec(memory_space=pltpu.VMEM)] * outputs,
        scratch_shapes=[pltpu.SemaphoreType.DMA((2 * outputs,))],
        cost_estimate=pl.CostEstimate(
            flops=0, transcendentals=0, bytes_accessed=8 * outputs * count * auxiliary
        ),
        compiler_params=pltpu.CompilerParams(vmem_limit_bytes=limit),
        name="take_pairs",
    )(index, source)


def start_all(copies):
    for copy in copies:
        copy.start()


def load_sets(sets, meta_ref, part_refs, buffers, sem):
    copies, part_refs = [], iter(part_refs)
    for (base, _, _, counts), buffer in zip(sets, buffers):
        loads, row = [], 0
        for count in counts:
            part_ref = next(part_refs)
            for r in range(2):
                slot = r if part_ref.shape[0] == 2 else meta_ref[base + r]
                target = buffer.at[r, pl.ds(row, count), :]
                number = sum(len(c) for c in copies) + len(loads)
                loads.append(pltpu.make_async_copy(part_ref.at[slot], target, sem.at[number]))
            row += count
        copies.append(loads)
    return copies


def add_sets(sets, copies, buffers, steps, meta_ref, energy_ref, factors_ref, density_ref):
    for (base, group, first, counts), loads, buffer in zip(sets, copies, buffers):
        for copy in loads:
            copy.wait()
        for k in range(steps):

            @pl.when(meta_ref[base + 2 + 3 * k] > 0)
            def _():
                lmo, rank = meta_ref[base + 3 + 3 * k], meta_ref[base + 4 + 3 * k]
                energy = energy_ref[group]
                own_energy = jnp.broadcast_to(energy[k : k + 1], (8, energy.shape[1])).T[:, :1]
                other = energy[steps + k : steps + k + 1, first : first + sum(counts)]
                part = buffer[rank]
                integral = lax.dot_general(
                    factors_ref[lmo], part, (((1,), (1,)), ((), ())), preferred_element_type=F32
                )
                amplitude = (integral / (own_energy + other)).astype(BF16)
                density_ref[lmo] += jnp.dot(amplitude, part, preferred_element_type=F32)


def pair_kernel(sets, steps, initial, meta_ref, energy_ref, factors_ref, *refs):
    count = sum(len(counts) for *_, counts in sets)
    part_refs, refs = refs[:count], refs[count if initial else count + 1 :]
    density_ref, buffers, sem = refs[0], refs[1:-1], refs[-1]
    copies = load_sets(sets, meta_ref, part_refs, buffers, sem)
    for loads in copies:
        start_all(loads)
    if initial:
        density_ref[...] = jnp.zeros_like(density_ref)
    add_sets(sets, copies, buffers, steps, meta_ref, energy_ref, factors_ref, density_ref)


def set_shapes(sets, steps):
    static = tuple(
        ((2 + 3 * steps) * group, group, first, tuple(part.shape[1] for part in parts))
        for group, parts, first in sets
    )
    return static, [part for _, parts, _ in sets for part in parts]


def set_scratch(static, auxiliary):
    count = sum(2 * len(counts) for *_, counts in static)
    return [
        pltpu.VMEM((2, sum(counts), auxiliary), BF16) for *_, counts in static
    ], pltpu.SemaphoreType.DMA((count,))


def pair_terms(meta, energy, factors, sets, density):
    lmo_dev, orbitals, auxiliary = factors.shape
    steps = lmo_dev // 2
    static, parts = set_shapes(sets, steps)
    initial = density is None
    buffers, sem = set_scratch(static, auxiliary)
    any_spec = pl.BlockSpec(memory_space=pl.ANY)
    vmem_spec = pl.BlockSpec(memory_space=pltpu.VMEM)
    return pl.pallas_call(
        functools.partial(pair_kernel, static, steps, initial),
        out_shape=pltpu.VMEM((lmo_dev, orbitals, auxiliary), F32),
        in_specs=[pl.BlockSpec(memory_space=pltpu.SMEM), vmem_spec, vmem_spec]
        + [any_spec] * len(parts)
        + ([] if initial else [vmem_spec]),
        out_specs=vmem_spec,
        scratch_shapes=buffers + [sem],
        input_output_aliases={} if initial else {3 + len(parts): 0},
        cost_estimate=pl.CostEstimate(
            flops=4 * len(sets) * steps * orbitals * orbitals * auxiliary,
            transcendentals=len(sets) * steps * orbitals * orbitals,
            bytes_accessed=4 * len(sets) * orbitals * auxiliary,
        ),
        compiler_params=pltpu.CompilerParams(vmem_limit_bytes=VMEM_LIMIT),
        name="pair_terms",
    )(meta, energy, factors, *parts, *([] if initial else [density]))


def is_last_lmo(base, steps, meta_ref, lmo):
    return functools.reduce(
        jnp.logical_or, [meta_ref[base + 3 + 3 * k] == lmo for k in range(steps)]
    )


def add_total(total, integral, density):
    total[...] += lax.dot_general(
        integral, density.astype(BF16), (((0,), (0,)), ((), ())), preferred_element_type=F32
    )


def partial_kernel(base, steps, meta_ref, integrals_ref, density_ref, total_ref):
    total_ref[...] = jnp.zeros_like(total_ref)
    for i in range(density_ref.shape[0]):

        @pl.when(jnp.logical_not(is_last_lmo(base, steps, meta_ref, i)))
        def _():
            add_total(total_ref, integrals_ref[i], density_ref[i])


def partial_total(meta, group, density, integrals):
    lmo_dev, orbitals, auxiliary = density.shape
    steps = lmo_dev // 2
    vmem_spec = pl.BlockSpec(memory_space=pltpu.VMEM)
    return pl.pallas_call(
        functools.partial(partial_kernel, (2 + 3 * steps) * group, steps),
        out_shape=pltpu.VMEM((auxiliary, auxiliary), F32),
        in_specs=[pl.BlockSpec(memory_space=pltpu.SMEM), vmem_spec, vmem_spec],
        out_specs=vmem_spec,
        cost_estimate=pl.CostEstimate(
            flops=lmo_dev * orbitals * auxiliary * auxiliary,
            transcendentals=0,
            bytes_accessed=integrals.size,
        ),
        compiler_params=pltpu.CompilerParams(vmem_limit_bytes=VMEM_LIMIT),
        name="partial_total",
    )(meta, integrals, density)


def dense_tiles(total, first, wide_count):
    rows = total.shape[0] // wide_count
    whole_even, middle, whole_odd = [
        total[:, first + 128 * j : first + 128 * (j + 1)].reshape(wide_count, rows, 128)
        for j in range(3)
    ]
    upper, lower = middle[:, : rows // 2], middle[:, rows // 2 :]
    left = lax.broadcasted_iota(jnp.int32, upper.shape, 2) < 64
    half_even = jnp.where(left, upper, pltpu.roll(lower, 64, axis=2))
    half_odd = jnp.where(left, pltpu.roll(upper, 64, axis=2), lower)
    return (
        jnp.concatenate([whole_even, half_even], axis=1),
        jnp.concatenate([whole_odd, half_odd], axis=1),
    )


def sparse_tile(dense, odd):
    rows = dense.shape[0] * 2 // 3
    whole = dense[:rows]
    half = jnp.concatenate([dense[rows:, :64], dense[rows:, 64:]], axis=0)
    return jnp.where(
        odd, jnp.concatenate([half, whole], axis=1), jnp.concatenate([whole, half], axis=1)
    )


def finish_kernel(sets, steps, slab, meta_ref, parity_ref, energy_ref, factors_ref, *refs):
    count = sum(len(counts) for *_, counts in sets)
    part_refs, refs = refs[:count], refs[count:]
    _, integrals_ref, _, keep_ref, send_ref, density_ref, total = refs[:7]
    buffers, sem = refs[7:-1], refs[-1]
    copies = load_sets(sets, meta_ref, part_refs, buffers, sem)
    for group in copies:
        start_all(group)
    add_sets(sets, copies, buffers, steps, meta_ref, energy_ref, factors_ref, density_ref)
    for k in range(steps):
        lmo = meta_ref[sets[0][0] + 3 + 3 * k]
        add_total(total, integrals_ref[lmo], density_ref[lmo])
    value = total[...]
    total[...] = 0.5 * (value + value.T)
    parity = parity_ref[0]
    for q in range(keep_ref.shape[0]):
        if keep_ref.ndim == 3:
            keep_ref[q] = total[pl.ds((2 * q + parity) * slab, slab), :]
            send_ref[q] = total[pl.ds((2 * q + 1 - parity) * slab, slab), :].astype(BF16)
            continue
        even, odd = dense_tiles(total, 2 * q * slab, keep_ref.shape[1])

        @pl.when(parity == 0)
        def _():
            keep_ref[q] = even
            send_ref[q] = odd.astype(BF16)

        @pl.when(parity == 1)
        def _():
            keep_ref[q] = odd
            send_ref[q] = even.astype(BF16)


def finish(meta, parity, energy, factors, sets, density, integrals, total, counts):
    lmo_dev, orbitals, auxiliary = density.shape
    steps = lmo_dev // 2
    static, parts = set_shapes(sets, steps)
    wide_count, narrow_count = counts
    slab, rows = auxiliary // narrow_count, auxiliary // wide_count
    out = (narrow_count // 2, slab, auxiliary)
    if slab == 192 and rows % 32 == 0:
        out = (narrow_count // 2, wide_count, rows * slab // 128, 128)
    buffers, sem = set_scratch(static, auxiliary)
    vmem_spec = pl.BlockSpec(memory_space=pltpu.VMEM)
    smem_spec = pl.BlockSpec(memory_space=pltpu.SMEM)
    return pl.pallas_call(
        functools.partial(finish_kernel, static, steps, slab),
        out_shape=[
            pltpu.VMEM(out, F32),
            pltpu.VMEM(out, BF16),
            pltpu.VMEM(density.shape, F32),
            pltpu.VMEM(total.shape, F32),
        ],
        in_specs=[smem_spec, smem_spec, vmem_spec, vmem_spec]
        + [vmem_spec] * len(parts)
        + [vmem_spec] * 3,
        out_specs=[vmem_spec] * 4,
        scratch_shapes=buffers + [sem],
        input_output_aliases={4 + len(parts): 2, 6 + len(parts): 3},
        cost_estimate=pl.CostEstimate(
            flops=2 * lmo_dev * orbitals * auxiliary * auxiliary,
            transcendentals=0,
            bytes_accessed=6 * density.size,
        ),
        compiler_params=pltpu.CompilerParams(vmem_limit_bytes=VMEM_LIMIT),
        name="finish",
    )(meta, parity, energy, factors, *parts, density, integrals, total)[:2]


def halve(x, axis, bit, high, dim):
    pairs = x.reshape(x.shape[:dim] + (x.shape[dim] // 2, 2) + x.shape[dim + 1 :])
    first, second = [lax.index_in_dim(pairs, b, dim + 1, keepdims=False) for b in range(2)]
    keep = jnp.where(high, second, first)
    send = jnp.where(high, first, second).astype(BF16)
    return keep + xor_permute(send, axis, bit).astype(F32)


def bits_of(count):
    return [1 << b for b in range(count.bit_length() - 1)]


def local(factors, integrals, pao_energy, lmo_energy, partners):
    wide_count = lax.axis_size("wide")
    narrow_count = lax.axis_size("narrow")
    wide_index = lax.axis_index("wide")
    narrow_index = lax.axis_index("narrow")
    lmo_dev, orbitals, auxiliary = factors.shape
    pair_count = lmo_dev * PARTNERS
    group_pairs = lmo_dev // 2
    half = wide_count // 2
    chunk, direct = [orbitals * c // 256 // 16 * 16 for c in MIRRORED_ROWS]

    leading = factors[:, :chunk]
    leading, others = lax.optimization_barrier((leading, factors))
    mirrored = [xor_permute(x, "wide", half) for x in [leading, others[:, chunk:direct]]]

    column = lax.dynamic_index_in_dim(
        partners.reshape(wide_count, narrow_count, pair_count), narrow_index, 1, keepdims=False
    )
    groups = column // lmo_dev // narrow_count
    slots = column % lmo_dev
    ids = jnp.arange(wide_count, dtype=jnp.int32)
    hit = groups[:, :, None] == ids
    low = jnp.min(jnp.where(hit, slots[:, :, None], lmo_dev - 1), axis=1)
    high = jnp.max(jnp.where(hit, slots[:, :, None], 0), axis=1)
    asked = jnp.stack([low, high], axis=-1)
    order = wide_index ^ ids
    by_order = (order[:, None] == ids)[:, :, None]

    def asked_of(group):
        listed = lax.dynamic_index_in_dim(asked, group, 1, keepdims=False)
        return jnp.sum(jnp.where(by_order, listed[None], 0), axis=1, dtype=jnp.int32)

    asked = jnp.stack([asked_of(wide_index), asked_of(wide_index ^ half)]).reshape(-1)

    limit = (64 << 20) - (3 << 19)
    offsets = tuple(range(2, half)) + (1,)
    near = [None] * (half - 1)
    for d, x in zip(offsets, take_near(factors, partners, offsets, limit)):
        near[d - 1] = xor_permute(x, "wide", d)
    far_asked, mirrored[0] = lax.optimization_barrier((asked, mirrored[0]))
    far_rows = list(take_pairs(factors, far_asked, 2 * half, half, direct, orbitals - direct))
    late = half // 2
    forwarded = [
        [
            xor_permute(x, "wide", d + 1)
            for d, x in enumerate(take_pairs(m, asked, 2 * wide_count + 2, half - 1, 0, m.shape[1]))
        ]
        for m in mirrored
    ]

    far = [xor_permute(x, "wide", half + d) for d, x in enumerate(far_rows)]

    own_groups = lax.dynamic_index_in_dim(groups, wide_index, 0, keepdims=False)
    own_slots = lax.dynamic_index_in_dim(slots, wide_index, 0, keepdims=False)
    listed = lax.dynamic_index_in_dim(column, wide_index, 0, keepdims=False)
    own_low = lax.dynamic_index_in_dim(low, wide_index, 0, keepdims=False)
    own_high = lax.dynamic_index_in_dim(high, wide_index, 0, keepdims=False)
    pair_ids = jnp.arange(pair_count, dtype=jnp.int32)
    place = jnp.sum(
        (own_groups[:, None] == own_groups[None, :]) & (pair_ids[None, :] < pair_ids[:, None]),
        axis=1, dtype=jnp.int32,
    )
    steps = jnp.arange(group_pairs, dtype=jnp.int32)
    picked = (own_groups == order[:, None, None]) & (place == steps[None, :, None])

    def of_pair(values):
        return jnp.sum(jnp.where(picked, values, 0), axis=2, dtype=jnp.int32)

    valid = of_pair(jnp.ones_like(pair_ids))
    lmo = jnp.where(valid > 0, of_pair(pair_ids // PARTNERS), steps)
    lowest = jnp.sum(jnp.where(own_groups[:, None] == ids, own_low, 0), axis=1, dtype=jnp.int32)
    rank = of_pair((own_slots > lowest).astype(jnp.int32))
    bounds = jnp.stack([own_low, own_high], axis=-1)
    bounds = jnp.sum(jnp.where(by_order, bounds[None], 0), axis=1, dtype=jnp.int32)
    triples = jnp.stack([valid, lmo, rank], axis=-1).reshape(wide_count, 3 * group_pairs)
    meta = jnp.concatenate([bounds, triples], axis=1).reshape(-1)

    shifted = pao_energy - lmo_energy[:, None]
    first_lmo = (wide_index * narrow_count + narrow_index) * lmo_dev
    rows = jnp.concatenate([first_lmo + lmo, of_pair(listed)], axis=1)
    rows = jnp.pad(rows, ((0, 0), (0, -rows.shape[1] % 8)))
    energy = shifted.at[rows].get(mode="promise_in_bounds")

    highs = {("narrow", bit): (narrow_index & bit) > 0 for bit in bits_of(narrow_count)}
    highs |= {("wide", bit): (wide_index & bit) > 0 for bit in bits_of(wide_count)}
    parity = (narrow_index & 1).astype(jnp.int32).reshape(1)
    meta, parity, energy, highs = lax.optimization_barrier((meta, parity, energy, highs))

    def add(sets, density):
        return pair_terms(meta, energy, factors, sets, density)

    def far_set(d):
        parts = list(mirrored) if d == 0 else [pieces[d - 1] for pieces in forwarded]
        return half + d, parts + [far[d]], 0

    density = add([(0, [factors], 0)], None)
    density = add([(d, [near[d - 1]], 0) for d in range(1, half)], density)
    density = add([far_set(d) for d in range(late)], density)
    density = add([far_set(d) for d in range(late, half - 1)], density)
    total = partial_total(meta, wide_count - 1, density, integrals)
    keep, send = finish(
        meta, parity, energy, factors,
        [far_set(half - 1)], density, integrals, total,
        (wide_count, narrow_count),
    )

    x = keep + xor_permute(send, "narrow", 1).astype(F32)
    tile = (auxiliary // wide_count, auxiliary // narrow_count)
    packed = x.ndim == 4
    if not packed:
        x = x.transpose(0, 2, 1)
    x = x.reshape(narrow_count // 2, 2, half, tile[0] * tile[1] // 128, 128)
    y_bits = [("narrow", bit) for bit in bits_of(narrow_count)[1:]]
    x_bits = [("wide", bit) for bit in bits_of(wide_count)[: len(y_bits)]]
    paths = [x[:, 0], x[:, 1]]
    for step in range(2 * len(y_bits)):
        for p, order in enumerate([y_bits + x_bits, x_bits + y_bits]):
            axis, bit = order[step]
            paths[p] = halve(paths[p], axis, bit, highs[axis, bit], 0 if axis == "narrow" else 1)
    x = jnp.concatenate(paths, axis=1)[0]
    rest = bits_of(wide_count)[len(y_bits) :]
    for bit in rest:
        step = bit // rest[0]
        pairs = x.reshape((x.shape[0] // (2 * step), 2, step) + x.shape[1:])
        x = jnp.where(highs["wide", bit], pairs[:, ::-1], pairs).reshape(x.shape)
    total = x[0]
    for offset in range(x.shape[0] - 1, 0, -1):
        total += xor_permute(x[offset].astype(BF16), "wide", offset * rest[0]).astype(F32)
    x = total[None]
    return sparse_tile(x[0], highs["narrow", 1]) if packed else x[0].reshape(tile)


def solution(mesh):
    in_specs = (P(("wide", "narrow"), None, None), P(("wide", "narrow"), None, None), P(), P(), P())
    return jax.shard_map(
        local, mesh=mesh, in_specs=in_specs, out_specs=P("wide", "narrow"), check_vma=False
    )
```
